256 devices in a mesh: fac: 4 (over y_lo, core), col: 64 (over y_hi, x, z).
Axes of the slice: x: 4, y: 4 (y_hi: 2, y_lo: 2; y = y_hi * 2 + y_lo), z: 8, core: 2. Of those that a mesh axis runs over, the one named last changes fastest.
Arguments:
- lower_factor: bfloat16 [1, 4, 4, 256, 256], P(None, 'fac', None, None, 'col'), may hold values from -0.1875 to 0.1875
- panel_inverse: float32 [1, 4, 256, 256], P(None, 'fac', None, 'col'), may hold values from -0.375 to 0.375
- right_side: float32 [1, 4, 256, 8192], P(None, 'fac', None, 'col'), may hold values from -0.1875 to 0.1875
- fill: int32 [4, 4], replicated, may hold values 0 or 1
Outputs:
- schur: float32 [8192, 4, 2048], P('col', 'fac')
The draws below stay inside these ranges and needn't reach their ends.
All inputs are finite; a program needn't handle non-finite values.
Results may differ from the reference program's by a relative error of at most 0.0034.
Values may be sent and summed in bfloat16 or wider, within the bound.
No kernel may reach another device: no remote copies, remote signals or barrier semaphores. Data moves between devices by JAX's collectives and lax.ppermute only.
A program may use at most 64 MiB of HBM per device.

```python
import jax
import jax.numpy as jnp
from jax import lax

W = 256
MDEV = 128
PD = 1
P_SIZE = 4
M = 8192
N_FAC = 4
N_COL = 64


def touch_ends(array, stream_key, least, largest):
    extent = array.shape
    spot = [jax.random.randint(jax.random.fold_in(stream_key, axis), (), 0, extent[axis]) for axis in range(len(extent))]
    array = array.at[tuple(spot)].set(least)
    longest = extent.index(max(extent))
    spot[longest] = (spot[longest] + 1) % extent[longest]
    return array.at[tuple(spot)].set(largest)


def levels(key, dims, cuts, least, largest):
    def one(axis_at, shards_of):
        heights = jax.random.uniform(jax.random.fold_in(jax.random.fold_in(key, 6), axis_at), (shards_of,), jnp.float32, least / len(cuts), largest / len(cuts))
        return jnp.repeat(jnp.exp(heights), dims[axis_at] // shards_of).reshape((-1,) + (1,) * (len(dims) - axis_at - 1))

    loudness = one(*cuts[0])
    for cut in cuts[1:]:
        loudness = loudness * one(*cut)
    return loudness


def noise(own_key, dims, width, most, pieces=(), dtype=jnp.bfloat16):
    loudness = levels(own_key, dims, pieces, -0.22, 0.18) if pieces else 1.0
    drawn = jax.random.normal(own_key, dims, jnp.float32) * width * loudness
    return jnp.minimum(jnp.maximum(drawn, -most), most).astype(dtype)


def setup_inputs(seed: int = 0) -> dict:
    streams_of = jax.random.split(jax.random.key(seed), 5)
    lower_factor = noise(streams_of[0], (PD, N_FAC, P_SIZE, W, W), (P_SIZE * W) ** -0.5, 0.1875, ((1, 4), (4, 64)))
    panel_inverse = noise(streams_of[1], (PD, N_FAC, W, W), W ** -0.5, 0.375, ((1, 4), (3, 64)), jnp.float32)
    right_side = noise(streams_of[2], (PD, N_FAC, W, M), ((P_SIZE * W) ** -0.5), 0.1875, ((1, 4), (3, 64)), jnp.float32)
    fill = touch_ends((jax.random.randint(streams_of[3], (P_SIZE, P_SIZE), 0, 4) < 3).astype(jnp.int32), jax.random.fold_in(streams_of[3], 1), 0, 1)
    return {"lower_factor": lower_factor, "panel_inverse": panel_inverse, "right_side": right_side, "fill": fill}


def reference(lower_factor, panel_inverse, right_side, fill):
    blocks = lower_factor.reshape(P_SIZE, P_SIZE, W, W)
    inverses = panel_inverse.reshape(P_SIZE, W, W)
    pending = right_side.reshape(P_SIZE, W, M).astype(jnp.float32)
    solved_rows = []
    for step_index in range(P_SIZE):
        solve_now = jnp.dot(inverses[step_index], pending[step_index], precision=lax.Precision.HIGHEST, preferred_element_type=jnp.float32)
        rounded = solve_now.astype(jnp.bfloat16)
        solved_rows.append(rounded)
        if step_index + 1 < P_SIZE:
            column_mask = fill[step_index + 1:, step_index].astype(jnp.float32)
            later_blocks = blocks[step_index + 1:, step_index].astype(jnp.float32) * column_mask[:, None, None]
            update = jnp.einsum("nab,bm->nam", later_blocks, rounded.astype(jnp.float32))
            pending = pending.at[step_index + 1:].add(-update)
    solved = jnp.concatenate(solved_rows, axis=0)
    full = lax.dot_general(solved, solved, (((0,), (0,)), ((), ())), preferred_element_type=jnp.float32)
    arranged = full.reshape(M, N_COL, N_FAC, MDEV // N_FAC).transpose(0, 2, 1, 3)
    return arranged.reshape(M, N_FAC, M // N_FAC)
```

```python
import functools

import jax
import jax.numpy as jnp
from jax import lax
from jax.experimental import pallas as pl
from jax.experimental.pallas import tpu as pltpu
from jax.sharding import Mesh, PartitionSpec as P

FAC = ("yl", "core")
COL = ("yh", "x", "z")
NT = (((1,), (1,)), ((), ()))


def shift(a, axis, by):
    n = lax.axis_size(axis)
    return lax.ppermute(a, axis, [(i, (i + by) % n) for i in range(n)])


def spread(piece, axes):
    n = lax.axis_size(axes)
    return lax.all_to_all(
        jnp.broadcast_to(piece[None], (n,) + piece.shape), axes, 0, 0, tiled=True
    )


def ordered(mine, other, index):
    first = index == 0
    return jnp.where(first, mine, other), jnp.where(first, other, mine)


def final_kernel(z_ref, own_ref, *refs):
    blocks, out_ref, stage = refs[:-2], refs[-2], refs[-1]
    nz = len(blocks)
    for k in range(nz):
        stage[lax.rem(z_ref[0] + nz - k, nz)] = blocks[k][...]
    own = own_ref[...]
    groups, wide = stage.shape[1], nz * stage.shape[2]
    for g in range(groups):
        rhs = stage[:, g].reshape(wide, stage.shape[3])
        out_ref[:, g * wide : (g + 1) * wide] = lax.dot_general(
            own, rhs, NT, preferred_element_type=jnp.float32
        )


def per_device(lower_factor, panel_inverse, right_side, fill):
    w = panel_inverse.shape[2]
    fac = lax.axis_index(FAC)
    yl, core, z = (lax.axis_index(a) for a in ("yl", "core", "z"))
    nz = lax.axis_size("z")
    panels = fill.shape[0]

    d = panel_inverse[0, 0].T
    hi = lax.reduce_precision(d, 8, 7)
    lo = d - hi
    keep = lax.dynamic_slice_in_dim(fill, fac, 1, 0)[0, : panels - 1] == 1
    low = lower_factor[0, 0, : panels - 1].transpose(0, 2, 1)
    low = jnp.where(keep[:, None, None], low, jnp.zeros_like(low))
    rows = jnp.concatenate(
        [hi.astype(jnp.bfloat16)[None], lo.astype(jnp.bfloat16)[None], low], axis=0
    )
    kw = rows.shape[1]

    lower, upper = ordered(rows, shift(rows, "yl", 1), yl)
    piece = jnp.concatenate([lower[:3], upper], axis=0)
    got = spread(piece, COL)
    n_col = got.shape[0]
    got = got.transpose(1, 0, 2, 3).reshape(piece.shape[0], n_col * kw, w)
    even, odd = ordered(got, shift(got, "core", 1), core)

    def inverse(t, i):
        return t[i].astype(jnp.float32) + t[i + 1].astype(jnp.float32)

    inv = [inverse(even, 0), inverse(odd, 0), inverse(even, 3), inverse(odd, 3)]
    fact = {
        (1, 0): odd[2],
        (2, 0): even[5],
        (2, 1): even[6],
        (3, 0): odd[5],
        (3, 1): odd[6],
        (3, 2): odd[7],
    }

    b = lax.all_gather(right_side[0, 0].T, FAC, axis=0)
    solved = []
    for p in range(panels):
        r = b[p]
        for q in range(p):
            r = r - jnp.dot(
                solved[q], fact[p, q], preferred_element_type=jnp.float32
            )
        y = jnp.dot(
            r,
            inv[p],
            precision=lax.Precision.HIGHEST,
            preferred_element_type=jnp.float32,
        )
        solved.append(y.astype(jnp.bfloat16))
    own = jnp.concatenate(solved, axis=1)
    cols = own.shape[0]
    share = cols // panels
    mine = lax.dynamic_slice_in_dim(own, fac * share, share, 0)

    block = spread(mine, ("yh", "x"))
    ring = [None] * nz
    ring[0] = up = down = block
    for k in range(1, nz // 2 + 1):
        up = shift(up, "z", 1)
        ring[k] = up
        if k < nz // 2:
            down = shift(down, "z", -1)
            ring[nz - k] = down
    full = pl.pallas_call(
        final_kernel,
        out_shape=jax.ShapeDtypeStruct((cols, n_col * share), jnp.float32),
        in_specs=[pl.BlockSpec(memory_space=pltpu.SMEM)]
        + [pl.BlockSpec(memory_space=pltpu.VMEM)] * (nz + 1),
        out_specs=pl.BlockSpec(memory_space=pltpu.VMEM),
        scratch_shapes=[pltpu.VMEM((nz,) + block.shape, jnp.bfloat16)],
        name="product",
    )(z[None].astype(jnp.int32), own, *ring)
    return full[:, None, :]


def solution(mesh):
    fine = Mesh(mesh.devices.reshape(2, 2, 2, 4, 8), FAC + COL)
    return jax.shard_map(
        per_device,
        mesh=fine,
        in_specs=(
            P(None, FAC, None, None, COL),
            P(None, FAC, None, COL),
            P(None, FAC, None, COL),
            P(),
        ),
        out_specs=P(COL, FAC, None),
        check_vma=False,
    )
```

```python
import jax
import jax.numpy as jnp
from jax import lax
from jax.experimental import pallas as pl
from jax.experimental.pallas import tpu as pltpu
from jax.sharding import Mesh, PartitionSpec as P

FAC = ("yl", "core")
COL = ("yh", "x", "z")
NT = (((1,), (1,)), ((), ()))
BF = jnp.bfloat16
F32 = jnp.float32
LANES = 128


def shift(a, axis, by):
    n = lax.axis_size(axis)
    return lax.ppermute(a, axis, [(i, (i + by) % n) for i in range(n)])


def exchange(a, axes):
    return lax.all_to_all(a, axes, 0, 0, tiled=True)


def split(a):
    hi = lax.reduce_precision(a, 8, 7)
    return hi.astype(BF), (a - hi).astype(BF)


def dot(a, b):
    return jnp.dot(a, b, preferred_element_type=F32)


def solve_kernel(pos_ref, own_ref, other_ref, out_ref, mine_ref):
    peers, _, lanes = own_ref.shape
    half = peers // 2
    share = 32

    def run(pair, sections):
        def square(ref, yl, first):
            parts = [
                ref[yl * half : (yl + 1) * half, r : r + share, :].reshape(
                    half * share, lanes
                )
                for r in (first, first + share)
            ]
            return jnp.concatenate(parts, axis=1)

        solved = []
        for p in range(4):
            yl, core = divmod(p, 2)
            ref, section = pair[core], sections[core]
            base = 320 + section * 128
            r = square(ref, yl, base).astype(F32) + square(
                ref, yl, base + 64
            ).astype(F32)
            for q in range(p):
                r = r - dot(solved[q], square(ref, yl, 128 + 64 * q))
            rhi = r.astype(BF)
            rlo = (r - rhi.astype(F32)).astype(BF)
            dhi = square(ref, yl, 0)
            y = (dot(rlo, dhi) + dot(rhi, square(ref, yl, 64))) + dot(rhi, dhi)
            y = y.astype(BF)
            solved.append(y)
            out_ref[:, :, p * 256 : (p + 1) * 256] = y.reshape(half, share, 256)

    @pl.when(pos_ref[0] == 0)
    def _():
        run((own_ref, other_ref), (0, 1))

    @pl.when(pos_ref[0] == 1)
    def _():
        run((other_ref, own_ref), (1, 0))

    mine_ref[...] = out_ref[pos_ref[1]]


def final_kernel(pos_ref, m0, m1, m2, *refs):
    blocks, out_ref, own, stage = refs[:-3], refs[-3], refs[-2], refs[-1]
    nz = len(blocks)
    z, yl, core = pos_ref[0], pos_ref[1], pos_ref[2]
    share = m0.shape[0]
    own[2 * yl + core] = m0[...]
    own[2 * (1 - yl) + core] = m1[...]
    own[2 * yl + (1 - core)] = m2[0]
    own[2 * (1 - yl) + (1 - core)] = m2[1]
    for k in range(nz):
        stage[lax.rem(z + nz - k, nz)] = blocks[k][...]
    lhs = own[...].reshape(4 * share, own.shape[2])
    groups, wide = stage.shape[1], nz * share
    for g in range(groups):
        rhs = stage[:, g].reshape(wide, stage.shape[3])
        out_ref[:, 0, g * wide : (g + 1) * wide] = lax.dot_general(
            lhs, rhs, NT, preferred_element_type=F32
        )


def per_device(lower_factor, panel_inverse, right_side, fill):
    w, kw = panel_inverse.shape[2:]
    fac = lax.axis_index(FAC)
    yl, core, yh, x, z = (lax.axis_index(a) for a in FAC + COL)
    nz, nx = lax.axis_size("z"), lax.axis_size("x")
    panels = fill.shape[0]

    hi, lo = split(panel_inverse[0, 0].T)
    keep = lax.dynamic_slice_in_dim(fill, fac, 1, 0)[0, : panels - 1] == 1
    low = lower_factor[0, 0, : panels - 1].transpose(0, 2, 1)
    low = jnp.where(keep[:, None, None], low, jnp.zeros_like(low))
    rows = jnp.concatenate([hi[None], lo[None], low], axis=0)
    nt = rows.shape[0]
    rows = rows.reshape(nt, kw, w // LANES, LANES).transpose(0, 2, 1, 3)
    rows = rows.reshape(nt * w // LANES * kw, LANES)
    got = exchange(jnp.broadcast_to(rows[None], (nz,) + rows.shape), "z")
    got = got.reshape(nz, nt * w // LANES, kw, LANES).transpose(1, 0, 2, 3)
    got = got.reshape(-1, LANES)

    share = right_side.shape[3] // panels
    bt = jnp.stack(split(right_side[0, 0].T))
    bt = bt.reshape(2, 2, 2, share, w // LANES, LANES).transpose(1, 2, 0, 4, 3, 5)
    bt = jnp.where(core == 0, bt, bt[:, ::-1]).reshape(2, -1, LANES)

    npeer = 2 * 2 * nx
    send = jnp.concatenate(
        [
            jnp.broadcast_to(got[None, None], (2, npeer // 2) + got.shape),
            jnp.broadcast_to(bt[:, None], (2, npeer // 2) + bt.shape[1:]),
        ],
        axis=2,
    ).reshape(npeer, -1, LANES)
    held = exchange(send, ("yl", "yh", "x"))
    other = shift(held, "core", 1)

    vm = pl.BlockSpec(memory_space=pltpu.VMEM)
    sm = pl.BlockSpec(memory_space=pltpu.SMEM)
    block, mine = pl.pallas_call(
        solve_kernel,
        out_shape=(
            jax.ShapeDtypeStruct((npeer // 2, share, panels * w), BF),
            jax.ShapeDtypeStruct((share, panels * w), BF),
        ),
        in_specs=[sm, vm, vm],
        out_specs=(vm, vm),
        name="solve",
    )(jnp.stack([core, yh * nx + x]).astype(jnp.int32), held, other)

    m1 = shift(mine, "yl", 1)
    m2 = shift(jnp.stack([mine, m1]), "core", 1)

    ring = [None] * nz
    ring[0] = up = down = block
    for k in range(1, nz // 2 + 1):
        up = shift(up, "z", 1)
        ring[k] = up
        if k < nz // 2:
            down = shift(down, "z", -1)
            ring[nz - k] = down
    return pl.pallas_call(
        final_kernel,
        out_shape=jax.ShapeDtypeStruct(
            (panels * share, 1, npeer // 2 * nz * share), F32
        ),
        in_specs=[sm] + [vm] * (nz + 3),
        out_specs=vm,
        scratch_shapes=[
            pltpu.VMEM((panels,) + mine.shape, BF),
            pltpu.VMEM((nz,) + block.shape, BF),
        ],
        name="product",
    )(jnp.stack([z, yl, core]).astype(jnp.int32), mine, m1, m2, *ring)


def solution(mesh):
    fine = Mesh(mesh.devices.reshape(2, 2, 2, 4, 8), FAC + COL)
    return jax.shard_map(
        per_device,
        mesh=fine,
        in_specs=(
            P(None, FAC, None, None, COL),
            P(None, FAC, None, COL),
            P(None, FAC, None, COL),
            P(),
        ),
        out_specs=P(COL, FAC, None),
        check_vma=False,
    )
```

```python
import jax
import jax.numpy as jnp
from jax import lax
from jax.experimental import pallas as pl
from jax.experimental.pallas import tpu as pltpu
from jax.sharding import Mesh, PartitionSpec as P


FAC = ("yl", "core")
COL = ("yh", "x", "z")
NT = (((1,), (1,)), ((), ()))
BF = jnp.bfloat16
F32 = jnp.float32
LANES = 128


def shift(a, axis, by=1):
    n = lax.axis_size(axis)
    return lax.ppermute(a, axis, [(i, (i + by) % n) for i in range(n)])


def opposite(a, axes):
    n = lax.axis_size(axes)
    return lax.ppermute(a, axes, [(i, n - 1 - i) for i in range(n)])


def exchange(a, axes):
    return lax.all_to_all(a, axes, 0, 0, tiled=True)


def by_index(mine, other, index):
    first = index == 0
    return jnp.stack([jnp.where(first, mine, other), jnp.where(first, other, mine)])


def split(a):
    hi = lax.reduce_precision(a, 8, 7)
    return hi.astype(BF), (a - hi).astype(BF)


def dot(a, b):
    return jnp.dot(a, b, preferred_element_type=F32)


def solve_panels(panels, pos_ref, own_ref, other_ref, rights, before, out_ref):
    peers, _, lanes = own_ref.shape
    half = peers // 2
    share, w = 32, rights.shape[3]

    def run(pair):
        def square(ref, yl, first):
            parts = [
                ref[yl * half : (yl + 1) * half, r : r + 32, :].reshape(
                    half * 32, lanes
                )
                for r in (first, first + 32)
            ]
            return jnp.concatenate(parts, axis=1)

        solved = [
            ref[:, :, i * w : (i + 1) * w].reshape(half * share, w)
            for ref in before
            for i in range(2)
        ]
        for n, p in enumerate(panels):
            yl, core = divmod(p, 2)
            ref = pair[core]
            r = rights[yl, core]
            for q in range(p):
                r = r - dot(solved[q], square(ref, yl, 128 + 64 * q))
            rhi = r.astype(BF)
            rlo = (r - rhi.astype(F32)).astype(BF)
            dhi = square(ref, yl, 0)
            y = (dot(rlo, dhi) + dot(rhi, square(ref, yl, 64))) + dot(rhi, dhi)
            y = y.astype(BF)
            solved.append(y)
            out_ref[:, :, n * w : (n + 1) * w] = y.reshape(half, share, w)

    @pl.when(pos_ref[0] == 0)
    def _():
        run((own_ref, other_ref))

    @pl.when(pos_ref[0] == 1)
    def _():
        run((other_ref, own_ref))


def first_kernel(pos_ref, own, other, rights, out_ref):
    solve_panels((0, 1), pos_ref, own, other, rights, (), out_ref)


def second_kernel(pos_ref, own, other, rights, a_ref, out_ref, mine_ref):
    solve_panels((2, 3), pos_ref, own, other, rights, (a_ref,), out_ref)
    wide = a_ref.shape[2]
    mine_ref[:, :wide] = a_ref[0]
    mine_ref[:, wide:] = out_ref[0]


def product_kernel(pos_ref, m0, m1, m2, *refs):
    blocks, out_ref, own, stage = refs[:-3], refs[-3], refs[-2], refs[-1]
    nz = stage.shape[0]
    z, yl, core, yh, x = (pos_ref[i] for i in range(5))
    share = m0.shape[0]
    own[2 * yl + core] = m0[...]
    own[2 * (1 - yl) + core] = m1[...]
    own[2 * yl + (1 - core)] = m2[0]
    own[2 * (1 - yl) + (1 - core)] = m2[1]
    groups = stage.shape[1]
    wide = stage.shape[3] // 2
    per = nz + 1
    for c in range(2):
        for k in range(per):
            src = blocks[c * per + k]
            if k < nz - 1:
                off = k if k < nz // 2 else nz // 2 - 1 - k
                part = slice(0, groups)
            else:
                off = nz // 2
                part = slice(0, groups // 2) if k == nz - 1 else slice(groups // 2, groups)
            stage[
                lax.rem(z + nz - off, nz), part, :, c * wide : (c + 1) * wide
            ] = src[...]
    lhs = own[...].reshape(4 * share, own.shape[2])
    cols = nz * share
    for g in range(groups):
        dyh, dx = divmod(g, 4)
        rhs = stage[:, g].reshape(cols, stage.shape[3])
        at = lax.rem(yh + dyh, 2) * 4 + lax.rem(x + dx, 4)
        out_ref[:, 0, pl.ds(pl.multiple_of(at * cols, cols), cols)] = lax.dot_general(
            lhs, rhs, NT, preferred_element_type=F32
        )


def z_ring(chunks):
    half = lax.axis_size("z") // 2
    ups = [[c] for c in chunks]
    downs = [[c] for c in chunks]
    for _ in range(1, half):
        for u, d in zip(ups, downs):
            u.append(shift(u[-1], "z", 1))
            d.append(shift(d[-1], "z", -1))
    out = []
    for u, d in zip(ups, downs):
        h = u[-1].shape[0] // 2
        last = [shift(u[-1][:h], "z", 1), shift(d[-1][h:], "z", -1)]
        out.extend(u + d[1:] + last)
    return out


def compute(lower_factor, panel_inverse, right_side, fill):
    w, kw = panel_inverse.shape[2:]
    fac = lax.axis_index(FAC)
    yl, core, yh, x, z = (lax.axis_index(a) for a in FAC + COL)
    nz, nx = lax.axis_size("z"), lax.axis_size("x")
    panels = fill.shape[0]

    hi, lo = split(panel_inverse[0, 0].T)
    keep = lax.dynamic_slice_in_dim(fill, fac, 1, 0)[0, : panels - 1] == 1
    low = lower_factor[0, 0, : panels - 1].transpose(0, 2, 1)
    low = jnp.where(keep[:, None, None], low, jnp.zeros_like(low))
    rows = jnp.concatenate([hi[None], lo[None], low], axis=0)
    nt = rows.shape[0]
    rows = rows.reshape(nt, kw, w // LANES, LANES).transpose(0, 2, 1, 3)
    rows = rows.reshape(nt * w // LANES * kw, LANES)
    rows = jnp.broadcast_to(rows[None], (nz,) + rows.shape)
    got = exchange(rows, "z")
    got = got.reshape(nz, nt * w // LANES, kw, LANES).transpose(1, 0, 2, 3)
    got = got.reshape(-1, LANES)
    npeer = 2 * 2 * nx
    got = jnp.broadcast_to(got[None], (npeer,) + got.shape)
    held = exchange(got, ("yl", "yh", "x"))
    other = shift(held, "core")

    share = right_side.shape[3] // panels
    bt = right_side[0, 0].T
    bo = shift(bt, "core")
    bt = by_index(bt, bo, core)
    bt = bt.reshape(2, 2, 2, share, w)
    bt = lax.dynamic_index_in_dim(bt, core, 2, keepdims=False)
    same = lax.dynamic_index_in_dim(bt, yl, 1, keepdims=False)
    cross = lax.dynamic_index_in_dim(bt, 1 - yl, 1, keepdims=False)
    near = jnp.stack([same, shift(same, "yh")])
    far = jnp.stack([shift(cross, "yl"), opposite(cross, ("yl", "yh"))])
    bt = by_index(near, far, yl)
    parts = [bt] + [shift(bt, "x", nx - k) for k in range(1, nx)]
    rights = jnp.stack(parts, axis=2).transpose(0, 3, 1, 2, 4, 5)
    rights = rights.reshape(2, 2, 2 * nx * share, w)

    vm = pl.BlockSpec(memory_space=pltpu.VMEM)
    sm = pl.BlockSpec(memory_space=pltpu.SMEM)
    pos = jnp.stack([core]).astype(jnp.int32)
    half = jax.ShapeDtypeStruct((npeer // 2, share, panels * w // 2), BF)
    params = pltpu.CompilerParams(vmem_limit_bytes=16 * 1024 * 1024)
    first = pl.pallas_call(
        first_kernel,
        out_shape=half,
        in_specs=[sm] + [vm] * 3,
        out_specs=vm,
        compiler_params=params,
        name="solve_a",
    )(pos, held, other, rights)
    second, mine = pl.pallas_call(
        second_kernel,
        out_shape=(half, jax.ShapeDtypeStruct((share, panels * w), BF)),
        in_specs=[sm] + [vm] * 4,
        out_specs=(vm, vm),
        compiler_params=params,
        name="solve_b",
    )(pos, held, other, rights, first)

    m1 = shift(mine, "yl")
    m2 = shift(jnp.stack([mine, m1]), "core")
    ring = z_ring([first, second])
    return pl.pallas_call(
        product_kernel,
        out_shape=jax.ShapeDtypeStruct(
            (panels * share, 1, npeer // 2 * nz * share), F32
        ),
        in_specs=[sm] + [vm] * (3 + len(ring)),
        out_specs=vm,
        scratch_shapes=[
            pltpu.VMEM((panels,) + mine.shape, BF),
            pltpu.VMEM((nz, npeer // 2, share, panels * w), BF),
        ],
        compiler_params=pltpu.CompilerParams(vmem_limit_bytes=20 * 1024 * 1024),
        name="product",
    )(jnp.stack([z, yl, core, yh, x]).astype(jnp.int32), mine, m1, m2, *ring)


def solution(mesh):
    fine = Mesh(mesh.devices.reshape(2, 2, 2, 4, 8), FAC + COL)
    return jax.shard_map(
        compute,
        mesh=fine,
        in_specs=(
            P(None, FAC, None, None, COL),
            P(None, FAC, None, COL),
            P(None, FAC, None, COL),
            P(),
        ),
        out_specs=P(COL, FAC, None),
        check_vma=False,
    )
```

```python
import jax
import jax.numpy as jnp
from jax import lax
from jax.experimental import pallas as pl
from jax.experimental.pallas import tpu as pltpu
from jax.sharding import Mesh, PartitionSpec as P


FAC = ("yl", "core")
COL = ("yh", "x", "z")
NT = (((1,), (1,)), ((), ()))
BF = jnp.bfloat16
F32 = jnp.float32
LANES = 128
MIB = 1024 * 1024


def shift(a, axis, by=1):
    n = lax.axis_size(axis)
    return lax.ppermute(a, axis, [(i, (i + by) % n) for i in range(n)])


def opposite(a, axes):
    n = lax.axis_size(axes)
    return lax.ppermute(a, axes, [(i, n - 1 - i) for i in range(n)])


def by_index(mine, other, index):
    first = index == 0
    return jnp.stack([jnp.where(first, mine, other), jnp.where(first, other, mine)])


def split(a):
    hi = lax.reduce_precision(a, 8, 7)
    return hi.astype(BF), (a - hi).astype(BF)


def dot(a, b):
    return jnp.dot(a, b, preferred_element_type=F32)


def solve_kernel(pos_ref, own_ref, twin_ref, rights, a_ref, b_ref, mine_ref):
    w = rights.shape[3]
    groups, share = a_ref.shape[:2]
    cut = groups * share

    def run(pair):
        solved = []
        for p in range(4):
            yl, core = divmod(p, 2)
            ref, base = pair[core], 3 * yl
            r = rights[yl, core]
            for q in range(p):
                r = r - dot(solved[q], ref[base + 2 + q])
            rhi = r.astype(BF)
            rlo = (r - rhi.astype(F32)).astype(BF)
            dhi = ref[base]
            y = (dot(rlo, dhi) + dot(rhi, ref[base + 1])) + dot(rhi, dhi)
            y = y.astype(BF)
            solved.append(y)
            at = slice(p * w, (p + 1) * w)
            a_ref[:, :, at] = y[:cut].reshape(groups, share, w)
            b_ref[:, :, at] = y[cut:].reshape(groups, share, w)
            mine_ref[:, at] = y[:share]

    @pl.when(pos_ref[0] == 0)
    def _():
        run((own_ref, twin_ref))

    @pl.when(pos_ref[0] == 1)
    def _():
        run((twin_ref, own_ref))


def product(lhs, chunks, place):
    n = 0
    for blocks in chunks:
        for g in range(blocks[0].shape[0]):
            rhs = jnp.concatenate([b[g] for b in blocks], axis=0)
            place(n, lax.dot_general(lhs, rhs, NT, preferred_element_type=F32))
            n += 1


def near_kernel(pos_ref, m0, m1, m2, *refs):
    blocks, out_ref, own = refs[:-2], refs[-2], refs[-1]
    yl, core = pos_ref[1], pos_ref[2]
    own[2 * yl + core] = m0[...]
    own[2 * (1 - yl) + core] = m1[...]
    own[2 * yl + (1 - core)] = m2[0]
    own[2 * (1 - yl) + (1 - core)] = m2[1]
    lhs = own[...].reshape(-1, own.shape[2])

    def place(g, value):
        out_ref[g] = value

    product(lhs, (blocks[:4], blocks[4:]), place)


def far_kernel(pos_ref, near, own, *refs):
    blocks, out_ref = refs[:-1], refs[-1]
    z, yh, x = pos_ref[0], pos_ref[3], pos_ref[4]
    lhs = own[...].reshape(-1, own.shape[2])
    cols = 2 * near.shape[2]
    turn = lax.rem(z + 6, 8) * (cols // 8)

    def place(g, value):
        full = jnp.concatenate([near[g], value], axis=1)
        full = pltpu.roll(full, turn, 1)
        dyh, dx = divmod(g, 4)
        at = lax.rem(yh + dyh, 2) * 4 + lax.rem(x + dx, 4)
        out_ref[:, 0, pl.ds(pl.multiple_of(at * cols, cols), cols)] = full

    product(lhs, (blocks[:4], blocks[4:]), place)


def z_ring(chunks):
    ups = [[c] for c in chunks]
    downs = [[c] for c in chunks]
    for _ in range(1, 4):
        for u, d in zip(ups, downs):
            u.append(shift(u[-1], "z", 1))
            d.append(shift(d[-1], "z", -1))
    last = [shift(ups[0][-1], "z", 1)]
    last.append(shift(downs[1][-1], "z", -1))
    return [
        {0: u[0], -1: u[1], -2: u[2], -3: u[3], 1: d[1], 2: d[2], 3: d[3], 4: end}
        for u, d, end in zip(ups, downs, last)
    ]


def compute(lower_factor, panel_inverse, right_side, fill):
    w, kw = panel_inverse.shape[2:]
    fac = lax.axis_index(FAC)
    yl, core, yh, x, z = (lax.axis_index(a) for a in FAC + COL)
    nx = lax.axis_size("x")
    panels = fill.shape[0]
    halves = w // LANES

    hi, lo = split(panel_inverse[0, 0].T)
    keep = lax.dynamic_slice_in_dim(fill, fac, 1, 0)[0, : panels - 1] == 1
    low = lower_factor[0, 0, : panels - 1].transpose(0, 2, 1)
    low = jnp.where(keep[:, None, None], low, jnp.zeros_like(low))
    rows = jnp.concatenate([hi[None], lo[None], low], axis=0)
    nt = rows.shape[0]
    rows = rows.reshape(nt, kw, halves, LANES).transpose(0, 2, 1, 3)
    rows = rows.reshape(-1, LANES)
    wide = ("yl",) + COL
    peers = lax.axis_size(wide)
    rows = jnp.broadcast_to(rows[None], (peers,) + rows.shape)
    got = lax.all_to_all(rows, wide, 0, 0, tiled=True)
    got = got.reshape(2, peers // 2, nt, halves, kw, LANES)
    got = got.transpose(0, 2, 1, 4, 3, 5).reshape(2, nt, w, w)
    held = jnp.concatenate([got[0, :3], got[1]], axis=0)
    twin = shift(held, "core")

    share = right_side.shape[3] // panels
    bt = right_side[0, 0].T
    bo = shift(bt, "core")
    bt = by_index(bt, bo, core)
    bt = bt.reshape(2, 2, 2, share, w)
    bt = lax.dynamic_index_in_dim(bt, core, 2, keepdims=False)
    same = lax.dynamic_index_in_dim(bt, yl, 1, keepdims=False)
    cross = lax.dynamic_index_in_dim(bt, 1 - yl, 1, keepdims=False)
    near = jnp.stack([same, shift(same, "yh")])
    far = jnp.stack([shift(cross, "yl"), opposite(cross, ("yl", "yh"))])
    bt = by_index(near, far, yl)
    after = shift(bt, "x", -1)
    before = shift(bt, "x", 1)
    second = shift(after, "x", -1)
    rights = jnp.stack([bt, after, second, before], axis=2)
    rights = rights.transpose(0, 3, 1, 2, 4, 5)
    rights = rights.reshape(2, 2, 2 * nx * share, w)

    vm = pl.BlockSpec(memory_space=pltpu.VMEM)
    sm = pl.BlockSpec(memory_space=pltpu.SMEM)
    params = pltpu.CompilerParams(vmem_limit_bytes=16 * MIB)
    pos = jnp.stack([core]).astype(jnp.int32)
    half = jax.ShapeDtypeStruct((nx, share, panels * w), BF)
    one, two, mine = pl.pallas_call(
        solve_kernel,
        out_shape=(half, half, jax.ShapeDtypeStruct((share, panels * w), BF)),
        in_specs=[sm] + [vm] * 3,
        out_specs=(vm, vm, vm),
        compiler_params=params,
        name="solve",
    )(pos, held, twin, rights)

    m1 = shift(mine, "yl")
    m2 = shift(jnp.stack([mine, m1]), "core")
    ring = z_ring([one, two])

    pos = jnp.stack([z, yl, core, yh, x]).astype(jnp.int32)
    groups = 2 * nx
    cols = panels * share
    part, own = pl.pallas_call(
        near_kernel,
        out_shape=(
            jax.ShapeDtypeStruct((groups, cols, 4 * share), F32),
            jax.ShapeDtypeStruct((panels, share, panels * w), BF),
        ),
        in_specs=[sm] + [vm] * 11,
        out_specs=(vm, vm),
        compiler_params=params,
        name="near",
    )(pos, mine, m1, m2, *(c[k] for c in ring for k in (-2, -1, 0, 1)))
    return pl.pallas_call(
        far_kernel,
        out_shape=jax.ShapeDtypeStruct((cols, 1, groups * 8 * share), F32),
        in_specs=[sm] + [vm] * 10,
        out_specs=vm,
        compiler_params=params,
        name="far",
    )(pos, part, own, *(c[k] for c in ring for k in (2, 3, 4, -3)))


def solution(mesh):
    fine = Mesh(mesh.devices.reshape(2, 2, 2, 4, 8), FAC + COL)
    return jax.shard_map(
        compute,
        mesh=fine,
        in_specs=(
            P(None, FAC, None, None, COL),
            P(None, FAC, None, COL),
            P(None, FAC, None, COL),
            P(),
        ),
        out_specs=P(COL, FAC, None),
        check_vma=False,
    )
```

```python
import jax
import jax.numpy as jnp
from jax import lax
from jax.experimental import pallas as pl
from jax.experimental.pallas import tpu as pltpu
from jax.sharding import Mesh, PartitionSpec as P


FAC = ("yl", "core")
COL = ("yh", "x", "z")
NT = (((1,), (1,)), ((), ()))
BF = jnp.bfloat16
F32 = jnp.float32
LANES = 128
MIB = 1024 * 1024


def shift(a, axis, by=1):
    n = lax.axis_size(axis)
    return lax.ppermute(a, axis, [(i, (i + by) % n) for i in range(n)])


def opposite(a, axes):
    n = lax.axis_size(axes)
    return lax.ppermute(a, axes, [(i, n - 1 - i) for i in range(n)])


def by_index(mine, other, index):
    first = index == 0
    return jnp.stack([jnp.where(first, mine, other), jnp.where(first, other, mine)])


def split(a):
    hi = lax.reduce_precision(a, 8, 7)
    return hi.astype(BF), (a - hi).astype(BF)


def dot(a, b):
    return jnp.dot(a, b, preferred_element_type=F32)


def solve_kernel(pos_ref, own_ref, twin_ref, pack, late, a_ref, b_ref, mine_ref):
    peers, _, lanes = own_ref.shape
    half = peers // 2
    share, w = pack.shape[4:]
    groups = a_ref.shape[0]
    cut = groups * share

    def square(ref, yl, block):
        parts = [
            ref[yl * half : (yl + 1) * half, r : r + 32, :].reshape(half * 32, lanes)
            for r in (64 * block, 64 * block + 32)
        ]
        return jnp.concatenate(parts, axis=1)

    def right(yl, core):
        rows = []
        for yh in range(2):
            rows += [pack[i, yl, yh, core] for i in range(4)]
            rows.append(late[yl, yh, core])
            rows += [pack[i, yl, yh, core] for i in range(4, 7)]
        return jnp.concatenate(rows, axis=0)

    def run(pair):
        solved = []
        for p in range(4):
            yl, core = divmod(p, 2)
            ref = pair[core]
            r = right(yl, core)
            for q in range(p):
                r = r - dot(solved[q], square(ref, yl, 2 + q))
            rhi = r.astype(BF)
            rlo = (r - rhi.astype(F32)).astype(BF)
            dhi = square(ref, yl, 0)
            y = (dot(rlo, dhi) + dot(rhi, square(ref, yl, 1))) + dot(rhi, dhi)
            y = y.astype(BF)
            solved.append(y)
            at = slice(p * w, (p + 1) * w)
            a_ref[:, :, at] = y[:cut].reshape(groups, share, w)
            b_ref[:, :, at] = y[cut:].reshape(groups, share, w)
            mine_ref[:, at] = y[:share]

    @pl.when(pos_ref[0] == 0)
    def _():
        run((own_ref, twin_ref))

    @pl.when(pos_ref[0] == 1)
    def _():
        run((twin_ref, own_ref))


def columns(lhs, block, z):
    nz, share, k = block.shape
    out = lax.dot_general(
        lhs, block[...].reshape(nz * share, k), NT, preferred_element_type=F32
    )
    return pltpu.roll(out, z * share, 1)


def near_kernel(pos_ref, m0, m1, m2, *refs):
    blocks, out_ref, own = refs[:-2], refs[-2], refs[-1]
    yl, core = pos_ref[1], pos_ref[2]
    own[2 * yl + core] = m0[...]
    own[2 * (1 - yl) + core] = m1[...]
    own[2 * yl + (1 - core)] = m2[0]
    own[2 * (1 - yl) + (1 - core)] = m2[1]
    lhs = own[...].reshape(-1, own.shape[2])
    for g, block in enumerate(blocks):
        out_ref[g] = columns(lhs, block, pos_ref[0])


def far_kernel(pos_ref, near, own, last0, last1, out_ref):
    z, yh, x = pos_ref[0], pos_ref[3], pos_ref[4]
    cols = near.shape[2]

    def place(dyh, dx, value):
        at = lax.rem(yh + dyh, 2) * 4 + lax.rem(x + dx, 4)
        out_ref[:, 0, pl.ds(pl.multiple_of(at * cols, cols), cols)] = value

    for dyh in range(2):
        for i, dx in enumerate((0, 1, 3)):
            place(dyh, dx, near[3 * dyh + i])
    lhs = own[...].reshape(-1, own.shape[2])
    for dyh, block in enumerate((last0, last1)):
        place(dyh, 2, columns(lhs, block, z))


def compute(lower_factor, panel_inverse, right_side, fill):
    w, kw = panel_inverse.shape[2:]
    fac = lax.axis_index(FAC)
    yl, core, yh, x, z = (lax.axis_index(a) for a in FAC + COL)
    nx = lax.axis_size("x")
    panels = fill.shape[0]
    halves = w // LANES

    hi, lo = split(panel_inverse[0, 0].T)
    keep = lax.dynamic_slice_in_dim(fill, fac, 1, 0)[0, : panels - 1] == 1
    low = lower_factor[0, 0, : panels - 1].transpose(0, 2, 1)
    low = jnp.where(keep[:, None, None], low, jnp.zeros_like(low))
    rows = jnp.concatenate([hi[None], lo[None], low], axis=0)
    nt = rows.shape[0]
    rows = rows.reshape(nt, kw, halves, LANES).transpose(0, 2, 1, 3)
    rows = rows.reshape(-1, LANES)
    nz = lax.axis_size("z")
    npeer = 2 * 2 * nx
    rows = jnp.broadcast_to(rows[None], (nz,) + rows.shape)
    got = lax.all_to_all(rows, "z", 0, 0, tiled=True)
    got = got.reshape(nz, nt * halves, kw, LANES).transpose(1, 0, 2, 3)
    got = got.reshape(-1, LANES)
    got = jnp.broadcast_to(got[None], (npeer,) + got.shape)
    held = lax.all_to_all(got, ("yl", "yh", "x"), 0, 0, tiled=True)
    twin = shift(held, "core")

    share = right_side.shape[3] // panels
    bt = right_side[0, 0].T
    bo = shift(bt, "core")
    bt = by_index(bt, bo, core)
    bt = bt.reshape(2, 2, 2, share, w)
    bt = lax.dynamic_index_in_dim(bt, core, 2, keepdims=False)
    same = lax.dynamic_index_in_dim(bt, yl, 1, keepdims=False)
    cross = lax.dynamic_index_in_dim(bt, 1 - yl, 1, keepdims=False)
    near = jnp.stack([same, shift(same, "yh")])
    far = jnp.stack([shift(cross, "yl"), opposite(cross, ("yl", "yh"))])
    bt = by_index(near, far, yl)
    ups, downs = [bt], [bt]
    for _ in range(1, 4):
        ups.append(shift(ups[-1], "z", 1))
        downs.append(shift(downs[-1], "z", -1))
    late = shift(ups[-1], "z", 1)
    pack = jnp.stack(downs + ups[:0:-1])

    vm = pl.BlockSpec(memory_space=pltpu.VMEM)
    sm = pl.BlockSpec(memory_space=pltpu.SMEM)
    params = pltpu.CompilerParams(vmem_limit_bytes=16 * MIB)
    pos = jnp.stack([core]).astype(jnp.int32)
    block = jax.ShapeDtypeStruct((nz, share, panels * w), BF)
    one, two, mine = pl.pallas_call(
        solve_kernel,
        out_shape=(block, block, jax.ShapeDtypeStruct((share, panels * w), BF)),
        in_specs=[sm] + [vm] * 4,
        out_specs=(vm, vm, vm),
        compiler_params=params,
        name="solve",
    )(pos, held, twin, pack, late)

    one_before, one_after = shift(one, "x", 1), shift(one, "x", -1)
    two_after, two_before = shift(two, "x", -1), shift(two, "x", 1)
    m1 = shift(mine, "yl")
    m2 = shift(jnp.stack([mine, m1]), "core")
    one_far = shift(one_before, "x", 1)
    two_far = shift(two_after, "x", -1)

    pos = jnp.stack([z, yl, core, yh, x]).astype(jnp.int32)
    cols = panels * share
    part, own = pl.pallas_call(
        near_kernel,
        out_shape=(
            jax.ShapeDtypeStruct((6, cols, nz * share), F32),
            jax.ShapeDtypeStruct((panels, share, panels * w), BF),
        ),
        in_specs=[sm] + [vm] * 9,
        out_specs=(vm, vm),
        compiler_params=params,
        name="near",
    )(pos, mine, m1, m2, one, one_after, one_before, two, two_after, two_before)
    return pl.pallas_call(
        far_kernel,
        out_shape=jax.ShapeDtypeStruct((cols, 1, 2 * nx * nz * share), F32),
        in_specs=[sm] + [vm] * 4,
        out_specs=vm,
        compiler_params=params,
        name="far",
    )(pos, part, own, one_far, two_far)


def solution(mesh):
    fine = Mesh(mesh.devices.reshape(2, 2, 2, 4, 8), FAC + COL)
    return jax.shard_map(
        compute,
        mesh=fine,
        in_specs=(
            P(None, FAC, None, None, COL),
            P(None, FAC, None, COL),
            P(None, FAC, None, COL),
            P(),
        ),
        out_specs=P(COL, FAC, None),
        check_vma=False,
    )
```

```python
import functools

import jax
import jax.numpy as jnp
from jax import lax
from jax.experimental import pallas as pl
from jax.experimental.pallas import tpu as pltpu
from jax.sharding import Mesh, PartitionSpec as P


FAC = ("yl", "core")
COL = ("yh", "x", "z")
NT = (((1,), (1,)), ((), ()))
BF = jnp.bfloat16
F32 = jnp.float32
LANES = 128
MIB = 1024 * 1024


def shift(a, axis, by=1):
    n = lax.axis_size(axis)
    return lax.ppermute(a, axis, [(i, (i + by) % n) for i in range(n)])


def by_index(mine, other, index):
    first = index == 0
    return jnp.stack([jnp.where(first, mine, other), jnp.where(first, other, mine)])


def split(a):
    hi = lax.reduce_precision(a, 8, 7)
    return hi.astype(BF), (a - hi).astype(BF)


def dot(a, b):
    return jnp.dot(a, b, preferred_element_type=F32)


def solve_kernel(pos_ref, own_ref, twin_ref, *refs):
    rights, late, outs = refs[:7], refs[7:9], refs[9:]
    peers, _, lanes = own_ref.shape
    half = peers // 2
    share, w = rights[0].shape[2:]

    def square(ref, yl, block):
        parts = [
            ref[yl * half : (yl + 1) * half, r : r + 32, :].reshape(half * 32, lanes)
            for r in (64 * block, 64 * block + 32)
        ]
        return jnp.concatenate(parts, axis=1)

    def right(yl, core):
        rows = [b[yl, core] for b in rights]
        rows.insert(4, late[yl][core])
        return jnp.concatenate(rows, axis=0)

    def factor(p, q):
        return ((0, 3) if q == 2 else (p // 2, 2 + q))

    def run(pair):
        solved = []
        for p in range(4):
            yl, core = divmod(p, 2)
            ref = pair[core]
            r = right(yl, core)
            for q in range(p):
                r = r - dot(solved[q], square(ref, *factor(p, q)))
            rhi = r.astype(BF)
            rlo = (r - rhi.astype(F32)).astype(BF)
            dhi = square(ref, yl, 0)
            y = (dot(rlo, dhi) + dot(rhi, square(ref, yl, 1))) + dot(rhi, dhi)
            y = y.astype(BF)
            solved.append(y)
            at = slice(p * w, (p + 1) * w)
            parts = y.reshape((2, -1, share, w))
            for i in range(2):
                outs[i][:, :, at] = parts[i]
            outs[2][:, at] = y[:share]

    @pl.when(pos_ref[0] == 0)
    def _():
        run((own_ref, twin_ref))

    @pl.when(pos_ref[0] == 1)
    def _():
        run((twin_ref, own_ref))


def columns(lhs, parts, z):
    nz, share, k = parts[0].shape
    rhs = jnp.concatenate([p[...].reshape(nz * share, k) for p in parts], axis=0)
    out = lax.dot_general(lhs, rhs, NT, preferred_element_type=F32)
    return pltpu.roll(out, z * share, 1)


NEAR = ((0, 0), (0, 1), (0, 3), (0, 2), (1, 0))
NEXT = ((1, 1), (1, 3))
LAST = ((1, 2),)


def near_kernel(pos_ref, m0, m1, m2, *refs):
    blocks, out_ref, own = refs[:-2], refs[-2], refs[-1]
    yl, core = pos_ref[1], pos_ref[2]
    own[2 * yl + core] = m0[...]
    own[2 * (1 - yl) + core] = m1[...]
    own[2 * yl + (1 - core)] = m2[0]
    own[2 * (1 - yl) + (1 - core)] = m2[1]
    lhs = own[...].reshape(-1, own.shape[2])
    for i, (dyh, dx) in enumerate(NEAR):
        value = columns(lhs, blocks[2 * i : 2 * i + 2], pos_ref[0])
        out_ref[:, 0, unit(pos_ref, dyh, dx, value.shape[1])] = value


def unit(pos_ref, dyh, dx, cols):
    at = lax.rem(pos_ref[3] + dyh, 2) * 4 + lax.rem(pos_ref[4] + dx, 4)
    return pl.ds(pl.multiple_of(at * cols, cols), cols)


def more_kernel(offsets, pos_ref, before, own, *refs):
    blocks, out_ref, stage, sems = refs[:-3], refs[-3], refs[-2], refs[-1]
    lhs = own[...].reshape(-1, own.shape[2])
    copies = []
    for i, (dyh, dx) in enumerate(offsets):
        stage[i, :, 0, :] = columns(lhs, blocks[2 * i : 2 * i + 2], pos_ref[0])
        at = unit(pos_ref, dyh, dx, stage.shape[3])
        copies.append(
            pltpu.make_async_copy(stage.at[i], out_ref.at[:, :, at], sems.at[i])
        )
        copies[-1].start()
    for copy in copies:
        copy.wait()


def y_shift(a, by):
    pairs = []
    for yl in range(2):
        for yh in range(2):
            y = (2 * yh + yl + by) % 4
            pairs.append((2 * yl + yh, 2 * (y % 2) + y // 2))
    return lax.ppermute(a, ("yl", "yh"), pairs)


def x_ring(halves):
    found = {0: halves}
    found[3] = [shift(h, "x", 1) for h in halves]
    found[1] = [shift(h, "x", -1) for h in halves]
    up = shift(found[3][0], "x", 1)
    down = shift(found[1][1], "x", -1)
    found[2] = [up, down]
    return found


def compute(lower_factor, panel_inverse, right_side, fill):
    w, kw = panel_inverse.shape[2:]
    fac = lax.axis_index(FAC)
    yl, core, yh, x, z = (lax.axis_index(a) for a in FAC + COL)
    nx = lax.axis_size("x")
    panels = fill.shape[0]
    halves = w // LANES

    hi, lo = split(panel_inverse[0, 0].T)
    keep = lax.dynamic_slice_in_dim(fill, fac, 1, 0)[0, : panels - 1] == 1
    low = lower_factor[0, 0, : panels - 1].transpose(0, 2, 1)
    low = jnp.where(keep[:, None, None], low, jnp.zeros_like(low))
    moved = shift(low[2], "yl")
    extra = jnp.where(yl == 0, moved, low[1])
    rows = jnp.stack([hi, lo, low[0], extra])
    nt = rows.shape[0]
    rows = rows.reshape(nt, kw, halves, LANES).transpose(0, 2, 1, 3)
    rows = rows.reshape(-1, LANES)
    nz = lax.axis_size("z")
    npeer = 2 * 2 * nx
    rows = jnp.broadcast_to(rows[None], (nz,) + rows.shape)
    got = lax.all_to_all(rows, "z", 0, 0, tiled=True)
    got = got.reshape(nz, nt * halves, kw, LANES).transpose(1, 0, 2, 3)
    got = got.reshape(-1, LANES)
    got = jnp.broadcast_to(got[None], (npeer,) + got.shape)
    held = lax.all_to_all(got, ("yl", "yh", "x"), 0, 0, tiled=True)
    twin = shift(held, "core")

    share = right_side.shape[3] // panels
    bt = right_side[0, 0].T
    bo = shift(bt, "core")
    bt = by_index(bt, bo, core)
    bt = bt.reshape(2, 2, 2, share, w)
    bt = lax.dynamic_index_in_dim(bt, core, 2, keepdims=False)
    same = lax.dynamic_index_in_dim(bt, yl, 1, keepdims=False)
    cross = lax.dynamic_index_in_dim(bt, 1 - yl, 1, keepdims=False)
    cross = shift(cross, "yl")
    bt = by_index(same, cross, yl)
    ups, downs = [bt], [bt]
    for _ in range(1, 4):
        ups.append(shift(ups[-1], "z", 1))
        downs.append(shift(downs[-1], "z", -1))
    late = shift(ups[-1][0], "z", 1), shift(downs[-1][1], "z", -1)
    rights = downs + ups[:0:-1]

    vm = pl.BlockSpec(memory_space=pltpu.VMEM)
    sm = pl.BlockSpec(memory_space=pltpu.SMEM)
    hbm = pl.BlockSpec(memory_space=pl.ANY)
    params = pltpu.CompilerParams(vmem_limit_bytes=16 * MIB)
    pos = jnp.stack([core]).astype(jnp.int32)
    part = jax.ShapeDtypeStruct((nz // 2, share, panels * w), BF)
    *solved, mine = pl.pallas_call(
        solve_kernel,
        out_shape=[part] * 2 + [jax.ShapeDtypeStruct((share, panels * w), BF)],
        in_specs=[sm] + [vm] * 11,
        out_specs=[vm] * 3,
        compiler_params=params,
        name="solve",
    )(pos, held, twin, *rights, *late)

    there = y_shift(solved[0], 1), y_shift(solved[1], -1)
    there = y_shift(there[0], 1), y_shift(there[1], -1)
    blocks = [x_ring(solved), x_ring(list(there))]
    m1 = shift(mine, "yl")
    m2 = shift(jnp.stack([mine, m1]), "core")

    def halves(offsets):
        return [half for dyh, dx in offsets for half in blocks[dyh][dx]]

    near = halves(NEAR)

    pos = jnp.stack([z, yl, core, yh, x]).astype(jnp.int32)
    cols = panels * share
    full = jax.ShapeDtypeStruct((cols, 1, 2 * nx * nz * share), F32)
    done, own = pl.pallas_call(
        near_kernel,
        out_shape=(full, jax.ShapeDtypeStruct((panels, share, panels * w), BF)),
        in_specs=[sm] + [vm] * (3 + len(near)),
        out_specs=(vm, vm),
        compiler_params=params,
        name="near",
    )(pos, mine, m1, m2, *near)

    def more(done, offsets):
        found = halves(offsets)
        n = len(offsets)
        return pl.pallas_call(
            functools.partial(more_kernel, offsets),
            out_shape=full,
            in_specs=[sm, hbm] + [vm] * (1 + len(found)),
            out_specs=hbm,
            input_output_aliases={1: 0},
            scratch_shapes=[
                pltpu.VMEM((n, cols, 1, nz * share), F32),
                pltpu.SemaphoreType.DMA((n,)),
            ],
            compiler_params=params,
        )(pos, done, own, *found)

    done = more(done, NEXT)
    return more(done, LAST)


def solution(mesh):
    fine = Mesh(mesh.devices.reshape(2, 2, 2, 4, 8), FAC + COL)
    return jax.shard_map(
        compute,
        mesh=fine,
        in_specs=(
            P(None, FAC, None, None, COL),
            P(None, FAC, None, COL),
            P(None, FAC, None, COL),
            P(),
        ),
        out_specs=P(COL, FAC, None),
        check_vma=False,
    )
```

```python
import functools

import jax
import jax.numpy as jnp
from jax import lax
from jax.experimental import pallas as pl
from jax.experimental.pallas import tpu as pltpu
from jax.sharding import Mesh, PartitionSpec as P


FAC = ("yl", "core")
COL = ("yh", "x", "z")
NT = (((1,), (1,)), ((), ()))
BF = jnp.bfloat16
F32 = jnp.float32
LANES = 128
MIB = 1024 * 1024


def shift(a, axis, by=1):
    n = lax.axis_size(axis)
    return lax.ppermute(a, axis, [(i, (i + by) % n) for i in range(n)])


def by_index(mine, other, index):
    first = index == 0
    return jnp.stack([jnp.where(first, mine, other), jnp.where(first, other, mine)])


def split(a):
    hi = lax.reduce_precision(a, 8, 7)
    return hi.astype(BF), (a - hi).astype(BF)


def dot(a, b):
    return jnp.dot(a, b, preferred_element_type=F32)


def solve_kernel(pos_ref, own_ref, twin_ref, *refs):
    rights, late, outs = refs[:7], refs[7], refs[8:]
    peers, _, lanes = own_ref.shape
    half = peers // 2
    share, w = rights[0].shape[2:]

    def square(ref, yl, block):
        parts = [
            ref[yl * half : (yl + 1) * half, r : r + 32, :].reshape(half * 32, lanes)
            for r in (64 * block, 64 * block + 32)
        ]
        return jnp.concatenate(parts, axis=1)

    def right(yl, core):
        rows = [b[yl, core] for b in rights]
        rows.insert(4, late[yl, core])
        return jnp.concatenate(rows, axis=0)

    def factor(p, q):
        return ((0, 3) if q == 2 else (p // 2, 2 + q))

    def run(pair):
        solved = []
        for p in range(4):
            yl, core = divmod(p, 2)
            ref = pair[core]
            r = right(yl, core)
            for q in range(p):
                r = r - dot(solved[q], square(ref, *factor(p, q)))
            rhi = r.astype(BF)
            rlo = (r - rhi.astype(F32)).astype(BF)
            dhi = square(ref, yl, 0)
            y = (dot(rlo, dhi) + dot(rhi, square(ref, yl, 1))) + dot(rhi, dhi)
            y = y.astype(BF)
            solved.append(y)
            at = slice(p * w, (p + 1) * w)
            parts = y.reshape((2, -1, share, w))
            for i in range(2):
                outs[i][:, :, at] = parts[i]
            outs[2][:, at] = y[:share]

    @pl.when(pos_ref[0] == 0)
    def _():
        run((own_ref, twin_ref))

    @pl.when(pos_ref[0] == 1)
    def _():
        run((twin_ref, own_ref))


def columns(lhs, parts, z):
    nz, share, k = parts[0].shape
    rhs = jnp.concatenate([p[...].reshape(nz * share, k) for p in parts], axis=0)
    out = lax.dot_general(lhs, rhs, NT, preferred_element_type=F32)
    return pltpu.roll(out, z * share, 1)


NEAR = ((0, 0), (0, 1), (0, 3), (0, 2), (1, 0))
NEXT = ((1, 1), (1, 3))
LAST = ((1, 2),)


def near_kernel(pos_ref, m0, m1, m2, *refs):
    blocks, out_ref, own = refs[:-2], refs[-2], refs[-1]
    yl, core = pos_ref[1], pos_ref[2]
    own[2 * yl + core] = m0[...]
    own[2 * (1 - yl) + core] = m1[...]
    own[2 * yl + (1 - core)] = m2[0]
    own[2 * (1 - yl) + (1 - core)] = m2[1]
    lhs = own[...].reshape(-1, own.shape[2])
    for i, (dyh, dx) in enumerate(NEAR):
        value = columns(lhs, blocks[2 * i : 2 * i + 2], pos_ref[0])
        out_ref[:, 0, unit(pos_ref, dyh, dx, value.shape[1])] = value


def unit(pos_ref, dyh, dx, cols):
    at = lax.rem(pos_ref[3] + dyh, 2) * 4 + lax.rem(pos_ref[4] + dx, 4)
    return pl.ds(pl.multiple_of(at * cols, cols), cols)


def more_kernel(offsets, pos_ref, before, own, *refs):
    blocks, out_ref, stage, sems = refs[:-3], refs[-3], refs[-2], refs[-1]
    lhs = own[...].reshape(-1, own.shape[2])
    copies = []
    for i, (dyh, dx) in enumerate(offsets):
        stage[i, :, 0, :] = columns(lhs, blocks[2 * i : 2 * i + 2], pos_ref[0])
        at = unit(pos_ref, dyh, dx, stage.shape[3])
        copies.append(
            pltpu.make_async_copy(stage.at[i], out_ref.at[:, :, at], sems.at[i])
        )
        copies[-1].start()
    for copy in copies:
        copy.wait()


def y_shift(a, by):
    pairs = []
    for yl in range(2):
        for yh in range(2):
            y = (2 * yh + yl + by) % 4
            pairs.append((2 * yl + yh, 2 * (y % 2) + y // 2))
    return lax.ppermute(a, ("yl", "yh"), pairs)


def x_ring(halves):
    found = {0: halves}
    found[3] = [shift(h, "x", 1) for h in halves]
    found[1] = [shift(h, "x", -1) for h in halves]
    up = shift(found[3][0], "x", 1)
    down = shift(found[1][1], "x", -1)
    found[2] = [up, down]
    return found


def compute(lower_factor, panel_inverse, right_side, fill):
    w, kw = panel_inverse.shape[2:]
    fac = lax.axis_index(FAC)
    yl, core, yh, x, z = (lax.axis_index(a) for a in FAC + COL)
    nx = lax.axis_size("x")
    panels = fill.shape[0]
    halves = w // LANES

    hi, lo = split(panel_inverse[0, 0].T)
    keep = lax.dynamic_slice_in_dim(fill, fac, 1, 0)[0, : panels - 1] == 1
    low = lower_factor[0, 0, : panels - 1].transpose(0, 2, 1)
    low = jnp.where(keep[:, None, None], low, jnp.zeros_like(low))
    moved = shift(low[2], "yl")
    extra = jnp.where(yl == 0, moved, low[1])
    rows = jnp.stack([hi, lo, low[0], extra])
    nt = rows.shape[0]
    rows = rows.reshape(nt, kw, halves, LANES).transpose(0, 2, 1, 3)
    rows = rows.reshape(-1, LANES)
    nz = lax.axis_size("z")
    npeer = 2 * 2 * nx
    rows = jnp.broadcast_to(rows[None], (nz,) + rows.shape)
    got = lax.all_to_all(rows, "z", 0, 0, tiled=True)
    got = got.reshape(nz, nt * halves, kw, LANES).transpose(1, 0, 2, 3)
    got = got.reshape(-1, LANES)
    got = jnp.broadcast_to(got[None], (npeer,) + got.shape)
    held = lax.all_to_all(got, ("yl", "yh", "x"), 0, 0, tiled=True)
    twin = shift(held, "core")

    share = right_side.shape[3] // panels
    bt = right_side[0, 0].T
    bo = shift(bt, "core")
    bt = by_index(bt, bo, core)
    bt = bt.reshape(2, 2, 2, share, w)
    bt = lax.dynamic_index_in_dim(bt, core, 2, keepdims=False)
    same = lax.dynamic_index_in_dim(bt, yl, 1, keepdims=False)
    cross = lax.dynamic_index_in_dim(bt, 1 - yl, 1, keepdims=False)
    cross = shift(cross, "yl")
    bt = by_index(same, cross, yl)
    ups, downs = [bt], [bt]
    for _ in range(1, 4):
        ups.append(shift(ups[-1], "z", 1))
        downs.append(shift(downs[-1], "z", -1))
    late = shift(ups[-1], "z", 1)
    rights = downs + ups[:0:-1]

    vm = pl.BlockSpec(memory_space=pltpu.VMEM)
    sm = pl.BlockSpec(memory_space=pltpu.SMEM)
    hbm = pl.BlockSpec(memory_space=pl.ANY)
    params = pltpu.CompilerParams(vmem_limit_bytes=16 * MIB)
    pos = jnp.stack([core]).astype(jnp.int32)
    part = jax.ShapeDtypeStruct((nz // 2, share, panels * w), BF)
    *solved, mine = pl.pallas_call(
        solve_kernel,
        out_shape=[part] * 2 + [jax.ShapeDtypeStruct((share, panels * w), BF)],
        in_specs=[sm] + [vm] * 10,
        out_specs=[vm] * 3,
        compiler_params=params,
        name="solve",
    )(pos, held, twin, *rights, late)

    there = y_shift(solved[0], 1), y_shift(solved[1], -1)
    there = y_shift(there[0], 1), y_shift(there[1], -1)
    blocks = [x_ring(solved), x_ring(list(there))]
    m1 = shift(mine, "yl")
    m2 = shift(jnp.stack([mine, m1]), "core")

    def halves(offsets):
        return [half for dyh, dx in offsets for half in blocks[dyh][dx]]

    near = halves(NEAR)

    pos = jnp.stack([z, yl, core, yh, x]).astype(jnp.int32)
    cols = panels * share
    full = jax.ShapeDtypeStruct((cols, 1, 2 * nx * nz * share), F32)
    done, own = pl.pallas_call(
        near_kernel,
        out_shape=(full, jax.ShapeDtypeStruct((panels, share, panels * w), BF)),
        in_specs=[sm] + [vm] * (3 + len(near)),
        out_specs=(vm, vm),
        compiler_params=params,
        name="near",
    )(pos, mine, m1, m2, *near)

    def more(done, offsets):
        found = halves(offsets)
        n = len(offsets)
        return pl.pallas_call(
            functools.partial(more_kernel, offsets),
            out_shape=full,
            in_specs=[sm, hbm] + [vm] * (1 + len(found)),
            out_specs=hbm,
            input_output_aliases={1: 0},
            scratch_shapes=[
                pltpu.VMEM((n, cols, 1, nz * share), F32),
                pltpu.SemaphoreType.DMA((n,)),
            ],
            compiler_params=params,
        )(pos, done, own, *found)

    done = more(done, NEXT)
    return more(done, LAST)


def solution(mesh):
    fine = Mesh(mesh.devices.reshape(2, 2, 2, 4, 8), FAC + COL)
    return jax.shard_map(
        compute,
        mesh=fine,
        in_specs=(
            P(None, FAC, None, None, COL),
            P(None, FAC, None, COL),
            P(None, FAC, None, COL),
            P(),
        ),
        out_specs=P(COL, FAC, None),
        check_vma=False,
    )
```

```python
import functools

import jax
import jax.numpy as jnp
from jax import lax
from jax.experimental import pallas as pl
from jax.experimental.pallas import tpu as pltpu
from jax.sharding import Mesh, PartitionSpec as P


FAC = ("yl", "core")
COL = ("yh", "x", "z")
NT = (((1,), (1,)), ((), ()))
BF = jnp.bfloat16
F32 = jnp.float32
LANES = 128
MIB = 1024 * 1024


def shift(a, axis, by=1):
    n = lax.axis_size(axis)
    return lax.ppermute(a, axis, [(i, (i + by) % n) for i in range(n)])


def by_index(mine, other, index):
    first = index == 0
    return jnp.stack([jnp.where(first, mine, other), jnp.where(first, other, mine)])


def split(a):
    hi = lax.reduce_precision(a, 8, 7)
    return hi.astype(BF), (a - hi).astype(BF)


def dot(a, b):
    return jnp.dot(a, b, preferred_element_type=F32)


def solve_kernel(pos_ref, own_ref, twin_ref, *refs):
    rights, late, outs = refs[:7], refs[7], refs[8:]
    peers, _, lanes = own_ref.shape
    half = peers // 2
    share, w = rights[0].shape[2:]

    def square(ref, yl, block):
        parts = [
            ref[yl * half : (yl + 1) * half, r : r + 32, :].reshape(half * 32, lanes)
            for r in (64 * block, 64 * block + 32)
        ]
        return jnp.concatenate(parts, axis=1)

    def right(yl, core):
        rows = [b[yl, core] for b in rights]
        rows.insert(4, late[yl, core])
        return jnp.concatenate(rows, axis=0)

    def factor(p, q):
        return ((0, 3) if q == 2 else (p // 2, 2 + q))

    def run(pair):
        solved = []
        for p in range(4):
            yl, core = divmod(p, 2)
            ref = pair[core]
            r = right(yl, core)
            for q in range(p):
                r = r - dot(solved[q], square(ref, *factor(p, q)))
            rhi = r.astype(BF)
            rlo = (r - rhi.astype(F32)).astype(BF)
            dhi = square(ref, yl, 0)
            y = (dot(rlo, dhi) + dot(rhi, square(ref, yl, 1))) + dot(rhi, dhi)
            y = y.astype(BF)
            solved.append(y)
            at = slice(p * w, (p + 1) * w)
            parts = y.reshape((2, -1, share, w))
            for i in range(2):
                outs[i][:, :, at] = parts[i]
            outs[2][:, at] = y[:share]

    @pl.when(pos_ref[0] == 0)
    def _():
        run((own_ref, twin_ref))

    @pl.when(pos_ref[0] == 1)
    def _():
        run((twin_ref, own_ref))


def columns(lhs, parts, z):
    nz, share, k = parts[0].shape
    rhs = jnp.concatenate([p[...].reshape(nz * share, k) for p in parts], axis=0)
    out = lax.dot_general(lhs, rhs, NT, preferred_element_type=F32)
    return pltpu.roll(out, z * share, 1)


NEAR = ((0, 0), (0, 1), (0, 3), (0, 2), (1, 0))
NEXT = ((1, 1), (1, 3))
LAST = ((1, 2),)


def near_kernel(pos_ref, m0, m1, m2, m3, *refs):
    blocks, out_ref, own = refs[:-2], refs[-2], refs[-1]
    yl, core = pos_ref[1], pos_ref[2]
    own[2 * yl + core] = m0[...]
    own[2 * (1 - yl) + core] = m1[...]
    own[2 * yl + (1 - core)] = m2[...]
    own[2 * (1 - yl) + (1 - core)] = m3[...]
    lhs = own[...].reshape(-1, own.shape[2])
    for i, (dyh, dx) in enumerate(NEAR):
        value = columns(lhs, blocks[2 * i : 2 * i + 2], pos_ref[0])
        out_ref[:, 0, unit(pos_ref, dyh, dx, value.shape[1])] = value


def unit(pos_ref, dyh, dx, cols):
    at = lax.rem(pos_ref[3] + dyh, 2) * 4 + lax.rem(pos_ref[4] + dx, 4)
    return pl.ds(pl.multiple_of(at * cols, cols), cols)


def more_kernel(offsets, pos_ref, before, own, *refs):
    blocks, out_ref, stage, sems = refs[:-3], refs[-3], refs[-2], refs[-1]
    lhs = own[...].reshape(-1, own.shape[2])
    copies = []
    for i, (dyh, dx) in enumerate(offsets):
        stage[i, :, 0, :] = columns(lhs, blocks[2 * i : 2 * i + 2], pos_ref[0])
        at = unit(pos_ref, dyh, dx, stage.shape[3])
        copies.append(
            pltpu.make_async_copy(stage.at[i], out_ref.at[:, :, at], sems.at[i])
        )
        copies[-1].start()
    for copy in copies:
        copy.wait()


def y_shift(a, by):
    pairs = []
    for yl in range(2):
        for yh in range(2):
            y = (2 * yh + yl + by) % 4
            pairs.append((2 * yl + yh, 2 * (y % 2) + y // 2))
    return lax.ppermute(a, ("yl", "yh"), pairs)


def x_ring(halves):
    found = {0: halves}
    found[3] = [shift(h, "x", 1) for h in halves]
    found[1] = [shift(h, "x", -1) for h in halves]
    up = shift(found[3][0], "x", 1)
    down = shift(found[1][1], "x", -1)
    found[2] = [up, down]
    return found


def compute(lower_factor, panel_inverse, right_side, fill):
    w, kw = panel_inverse.shape[2:]
    fac = lax.axis_index(FAC)
    yl, core, yh, x, z = (lax.axis_index(a) for a in FAC + COL)
    nx = lax.axis_size("x")
    panels = fill.shape[0]
    halves = w // LANES

    hi, lo = split(panel_inverse[0, 0].T)
    keep = lax.dynamic_slice_in_dim(fill, fac, 1, 0)[0, : panels - 1] == 1
    low = lower_factor[0, 0, : panels - 1].transpose(0, 2, 1)
    low = jnp.where(keep[:, None, None], low, jnp.zeros_like(low))
    moved = shift(low[2], "yl")
    extra = jnp.where(yl == 0, moved, low[1])
    rows = jnp.stack([hi, lo, low[0], extra])
    nt = rows.shape[0]
    rows = rows.reshape(nt, kw, halves, LANES).transpose(0, 2, 1, 3)
    rows = rows.reshape(-1, LANES)
    nz = lax.axis_size("z")
    npeer = 2 * 2 * nx
    rows = jnp.broadcast_to(rows[None], (nz,) + rows.shape)
    got = lax.all_to_all(rows, "z", 0, 0, tiled=True)
    got = got.reshape(nz, nt * halves, kw, LANES).transpose(1, 0, 2, 3)
    got = got.reshape(-1, LANES)
    got = jnp.broadcast_to(got[None], (npeer,) + got.shape)
    held = lax.all_to_all(got, ("yl", "yh", "x"), 0, 0, tiled=True)
    twin = shift(held, "core")

    share = right_side.shape[3] // panels
    bt = right_side[0, 0].T
    bo = shift(bt, "core")
    bt = by_index(bt, bo, core)
    bt = bt.reshape(2, 2, 2, share, w)
    bt = lax.dynamic_index_in_dim(bt, core, 2, keepdims=False)
    same = lax.dynamic_index_in_dim(bt, yl, 1, keepdims=False)
    cross = lax.dynamic_index_in_dim(bt, 1 - yl, 1, keepdims=False)
    cross = shift(cross, "yl")
    bt = by_index(same, cross, yl)
    ups, downs = [bt], [bt]
    for _ in range(1, 4):
        ups.append(shift(ups[-1], "z", 1))
        downs.append(shift(downs[-1], "z", -1))
    late = shift(ups[-1], "z", 1)
    rights = downs + ups[:0:-1]

    vm = pl.BlockSpec(memory_space=pltpu.VMEM)
    sm = pl.BlockSpec(memory_space=pltpu.SMEM)
    hbm = pl.BlockSpec(memory_space=pl.ANY)
    params = pltpu.CompilerParams(vmem_limit_bytes=16 * MIB)
    pos = jnp.stack([core]).astype(jnp.int32)
    part = jax.ShapeDtypeStruct((nz // 2, share, panels * w), BF)
    *solved, mine = pl.pallas_call(
        solve_kernel,
        out_shape=[part] * 2 + [jax.ShapeDtypeStruct((share, panels * w), BF)],
        in_specs=[sm] + [vm] * 10,
        out_specs=[vm] * 3,
        compiler_params=params,
        name="solve",
    )(pos, held, twin, *rights, late)

    there = y_shift(solved[0], 1), y_shift(solved[1], -1)
    there = y_shift(there[0], 1), y_shift(there[1], -1)
    blocks = [x_ring(solved), x_ring(list(there))]
    m1 = shift(mine, "yl")
    m2, m3 = shift(mine, "core"), shift(m1, "core")

    def halves(offsets):
        return [half for dyh, dx in offsets for half in blocks[dyh][dx]]

    near = halves(NEAR)

    pos = jnp.stack([z, yl, core, yh, x]).astype(jnp.int32)
    cols = panels * share
    full = jax.ShapeDtypeStruct((cols, 1, 2 * nx * nz * share), F32)
    done, own = pl.pallas_call(
        near_kernel,
        out_shape=(full, jax.ShapeDtypeStruct((panels, share, panels * w), BF)),
        in_specs=[sm] + [vm] * (4 + len(near)),
        out_specs=(vm, vm),
        compiler_params=params,
        name="near",
    )(pos, mine, m1, m2, m3, *near)

    def more(done, offsets):
        found = halves(offsets)
        n = len(offsets)
        return pl.pallas_call(
            functools.partial(more_kernel, offsets),
            out_shape=full,
            in_specs=[sm, hbm] + [vm] * (1 + len(found)),
            out_specs=hbm,
            input_output_aliases={1: 0},
            scratch_shapes=[
                pltpu.VMEM((n, cols, 1, nz * share), F32),
                pltpu.SemaphoreType.DMA((n,)),
            ],
            compiler_params=params,
        )(pos, done, own, *found)

    done = more(done, NEXT)
    return more(done, LAST)


def solution(mesh):
    fine = Mesh(mesh.devices.reshape(2, 2, 2, 4, 8), FAC + COL)
    return jax.shard_map(
        compute,
        mesh=fine,
        in_specs=(
            P(None, FAC, None, None, COL),
            P(None, FAC, None, COL),
            P(None, FAC, None, COL),
            P(),
        ),
        out_specs=P(COL, FAC, None),
        check_vma=False,
    )
```
